512 devices in a mesh: stream: 32 (over z, x_hi), span: 16 (over y, x_lo, core).
Axes of the slice: x: 4 (x_hi: 2, x_lo: 2; x = x_hi * 2 + x_lo), y: 4, z: 16, core: 2. Of those that a mesh axis runs over, the one named last changes fastest.
Arguments:
- checkpoint: float32 [5, 192, 32, 2048], P(None, None, 'stream', 'span'), may hold values from -4.8 to 4.8
- adjoint: float32 [5, 192, 32, 2048], P(None, None, 'stream', 'span'), may hold values from -6 to 6
- line_inverse: bfloat16 [32, 3, 320, 320], P('stream'), may hold values from -0.3125 to 0.3125
- row_source: int32 [3072], replicated, may hold values from 0 to 3071, as said below
Outputs:
- adjoint_start: float32 [5, 192, 32, 2048], P(None, None, 'stream', 'span')
The draws below stay inside these ranges and needn't reach their ends.
Inputs may be any that keep to these rules, and one draw needn't show every extreme that they name: `row_source`: every rotor outlet row is taken by exactly one stator inlet row, and each stator span tile takes exactly 12 rows from each rotor span tile.
All inputs are finite; a program needn't handle non-finite values.
Results may differ from the reference program's by a relative error of at most 0.0029.
Values sent between devices are 32-bit elements; how exact they have to be, the bound alone decides.
A program may use at most 64 MiB of HBM per device.

```python
import jax
import jax.numpy as jnp
from jax import lax

NC = 5
NL = 192
LB = 64
CP = 128
NB = 3
NS = 32
NP = 2048
SPLIT = 16
IROWS = 3072
CAP = 12
N_SPAN = 16


def draw_row_source(key, part):
    key_rows, key_mix = jax.random.split(jax.random.fold_in(key, 7))
    first_keys = jax.random.split(key_rows, N_SPAN)
    row_order = jax.vmap(lambda subkey: jax.random.permutation(subkey, NL))(first_keys).astype(jnp.int32)
    grouped = row_order.reshape(N_SPAN, N_SPAN, CAP)
    global_rows = grouped + (jnp.arange(N_SPAN, dtype=jnp.int32) * NL)[:, None, None]
    per_dest = jnp.transpose(global_rows, (1, 0, 2)).reshape(N_SPAN, NL)
    second_keys = jax.random.split(key_mix, N_SPAN)
    shuffle = jax.vmap(lambda subkey: jax.random.permutation(subkey, NL))(second_keys).astype(jnp.int32)
    shuffled_rows = jnp.take_along_axis(per_dest, shuffle, axis=1)
    return shuffled_rows.reshape(IROWS).astype(jnp.int32)


def shard_levels(key, shape, pieces, smallest, top_value):
    loudness = 1.0
    for axis_at, blocks in pieces:
        draws = jax.random.uniform(jax.random.fold_in(jax.random.fold_in(key, 6), axis_at), (blocks,), jnp.float32, smallest / len(pieces), top_value / len(pieces))
        loudness = loudness * jnp.repeat(jnp.exp(draws), shape[axis_at] // blocks).reshape((-1,) + (1,) * (len(shape) - 1 - axis_at))
    return loudness


def centred(own_key, extent, deviation, most, cuts=(), held_as=jnp.bfloat16):
    factor_of = shard_levels(own_key, extent, cuts, -0.22, 0.18) if cuts else 1.0
    values = jax.random.normal(own_key, extent, jnp.float32) * deviation * factor_of
    return jnp.minimum(jnp.maximum(values, -most), most).astype(held_as)


def setup_inputs(seed: int = 0) -> dict:
    splits = jax.random.split(jax.random.key(seed), 5)
    return {
        "checkpoint": centred(splits[0], (NC, NL, NS, NP), 0.8, 4.8, ((2, 32), (3, 16)), jnp.float32),
        "adjoint": centred(splits[1], (NC, NL, NS, NP), 1.0, 6.0, ((2, 32), (3, 16)), jnp.float32),
        "line_inverse": centred(splits[2], (NS, NB, NC * LB, NC * LB), (NC * LB) ** -0.5, 0.3125, ((0, 32),)),
        "row_source": draw_row_source(jax.random.fold_in(splits[4], 71), 0),
    }


time_step = 0.5
ADVECTION = (1.0, 0.6, 0.8, 1.2, 0.7)
DISSIPATION = (0.3, 0.25, 0.35, 0.3, 0.4)
SPREADING = (0.4, 0.3, 0.5, 0.35, 0.45)


def per_state(values):
    return jnp.array(values, jnp.float32).reshape(5, 1, 1, 1)


def shift_upstream(field, row_source):
    upstream = jnp.concatenate([jnp.zeros_like(field[:, :, :1]), field[:, :, :-1]], axis=2)
    face_rows = field[:, :, SPLIT - 1].reshape(NC, NL, N_SPAN, CP)
    src_dev = (row_source // NL).reshape(N_SPAN, NL)
    src_row = (row_source % NL).reshape(N_SPAN, NL)
    mapped = face_rows[:, src_row, src_dev, :]
    mapped = jnp.transpose(mapped, (0, 2, 1, 3)).reshape(NC, NL, NP)
    return upstream.at[:, :, SPLIT].set(mapped)


def shift_downstream(field, row_source):
    downstream = jnp.concatenate([field[:, :, 1:], jnp.zeros_like(field[:, :, :1])], axis=2)
    inverse_rows = jnp.zeros((IROWS,), jnp.int32).at[row_source].set(jnp.arange(IROWS, dtype=jnp.int32))
    inverse_rows = inverse_rows.reshape(N_SPAN, NL)
    face_rows = field[:, :, SPLIT].reshape(NC, NL, N_SPAN, CP)
    mapped = face_rows[:, inverse_rows % NL, inverse_rows // NL, :]
    mapped = jnp.transpose(mapped, (0, 2, 1, 3)).reshape(NC, NL, NP)
    return downstream.at[:, :, SPLIT - 1].set(mapped)


def operator(field, row_source, coef_down, coef_up, center, lateral):
    lateral_sum = jnp.roll(field, 1, axis=3) + jnp.roll(field, -1, axis=3) - 2.0 * field
    return (coef_down * shift_downstream(field, row_source) + coef_up * shift_upstream(field, row_source)
            + center * field + lateral * lateral_sum)


def reference(checkpoint, adjoint, line_inverse, row_source):
    advect = per_state(ADVECTION)
    dissip = per_state(DISSIPATION)
    lateral = per_state(SPREADING)
    toward_down = -0.5 * advect + dissip
    toward_up = 0.5 * advect + dissip
    center = -2.0 * dissip
    flux = jnp.tanh(checkpoint)
    advanced = checkpoint + time_step * operator(flux, row_source, toward_down, toward_up, center, lateral)
    tanh_adv = jnp.tanh(advanced)
    section_slope = 2.0 - tanh_adv * tanh_adv
    rounded = lax.optimization_barrier(adjoint.astype(jnp.bfloat16)).astype(jnp.float32)
    blocked = rounded.reshape(NC, NB, LB, NS, NP)
    inverse = line_inverse.astype(jnp.float32).reshape(NS, NB, NC, LB, NC, LB)
    carried = jnp.einsum('sbclem,cblsp->ebmsp', inverse, blocked,
                         precision=lax.Precision.HIGHEST).reshape(NC, NL, NS, NP)
    weighted = section_slope * carried
    tangent = 1.0 - flux * flux
    return weighted + time_step * tangent * operator(weighted, row_source, toward_up, toward_down, center, lateral)
```

```python
import jax
import jax.numpy as jnp
from jax import lax
from jax.experimental import pallas as pl
from jax.experimental.pallas import tpu as pltpu
from jax.sharding import PartitionSpec as P

time_step = 0.5
ADVECTION = (1.0, 0.6, 0.8, 1.2, 0.7)
DISSIPATION = (0.3, 0.25, 0.35, 0.3, 0.4)
SPREADING = (0.4, 0.3, 0.5, 0.35, 0.45)
MESH = pl.DeviceIdType.MESH
NC, NL, CP, NB, LB = 5, 192, 128, 3, 64
HALF = NL // 2
F32, BF16, I32 = jnp.float32, jnp.bfloat16, jnp.int32


def pick(values, index):
    out = jnp.float32(values[-1])
    for i in range(len(values) - 1):
        out = jnp.where(index == i, jnp.float32(values[i]), out)
    return out


def split(x):
    hi = x.astype(BF16)
    return hi, (x - hi.astype(F32)).astype(BF16)


def dot(a, b, dims):
    return lax.dot_general(a, b, (dims, ((), ())), preferred_element_type=F32)


def div_rows(x):
    return lax.shift_right_logical(x * 5462, 20)


def kernel(
    n_stream, n_span, ck_h, adj_h, li_h, rs_h, o_ref,
    cx, adj, li, rs, cb, fo, fld, hb, ob, eo, es, er, ys, yr, tm, tmt,
    l_sem, ck_s, ck_r, ca_s, ca_r, z_s, z_r, i_s, i_r, eo_s, eo_r, e_s, e_r, o_s, o_r, ready,
):
    s = lax.axis_index("stream")
    p = lax.axis_index("span")
    n_z = n_stream // 2
    zi = n_z // 2 - 1
    cap = NL // n_span
    pad = yr.shape[3]
    h = lax.rem(s, 2)
    z = s // 2
    slots = 3 - lax.rem(h + p, 2)
    other_slots = 5 - slots
    up_iface = z == zi
    down_iface = z == zi + 1
    iface = jnp.logical_or(up_iface, down_iface)
    has_up = z < n_z - 1
    has_down = z > 0
    send_up = jnp.logical_and(has_up, jnp.logical_not(up_iface))
    send_down = jnp.logical_and(has_down, jnp.logical_not(down_iface))
    s_face = 2 * jnp.where(up_iface, z + 1, z - 1)
    p_left = lax.rem(p + n_span - 1, n_span)
    p_right = lax.rem(p + 1, n_span)
    s_pair = s + 1 - 2 * h
    partner = {"stream": s_pair, "span": p}
    above = {"stream": lax.rem(s + 2, n_stream), "span": p}
    below = {"stream": lax.rem(s + n_stream - 2, n_stream), "span": p}

    def count(flag):
        return jnp.where(flag, 1, 0)

    def half(i):
        return pl.ds(pl.multiple_of(i * HALF, HALF), HALF)

    def mine(k):
        return jnp.where(k == 2, 2, 3 * h + k)

    def theirs(k):
        return jnp.where(k == 2, 2, 3 - 3 * h + k)

    def at(st, k):
        return jnp.where(h == st, mine(k), NC + k)

    def side_of(k, q):
        return jnp.where(k == 2, lax.rem(q, 2), h)

    def remote(src, dst, send, recv, device):
        return pltpu.make_async_remote_copy(
            src_ref=src, dst_ref=dst, send_sem=send, recv_sem=recv, device_id=device, device_id_type=MESH
        )

    local_ck = pltpu.make_async_copy(ck_h, cx.at[pl.ds(0, NC)], l_sem.at[0])
    local_adj = pltpu.make_async_copy(adj_h, adj, l_sem.at[1])
    local_li = pltpu.make_async_copy(li_h, li, l_sem.at[2])
    local_rs = pltpu.make_async_copy(rs_h, rs, l_sem.at[3])

    def send_ck(k):
        return remote(ck_h.at[theirs(k)], cx.at[NC + k], ck_s.at[k], ck_r.at[k], partner)

    def send_ca(k):
        return remote(cb.at[theirs(k)], cb.at[NC + k], ca_s.at[k], ca_r.at[k], partner)

    def send_out(k, c):
        return remote(ob.at[k], o_ref.at[c], o_s.at[k], o_r.at[k], partner)

    def field_up(f, k):
        return remote(fld.at[f, 2, k], fld.at[f, 0, k], z_s.at[f, k, 0], z_r.at[f, k, 0], above)

    def field_down(f, k):
        return remote(fld.at[f, 1, k], fld.at[f, 3, k], z_s.at[f, k, 1], z_r.at[f, k, 1], below)

    def own_edge(c, side):
        q = (p_right, p_left)[side]
        row = pl.ds(1 - side, 1)
        owner = jnp.where(c == 2, lax.rem(q, 2), c // 3)
        k = jnp.where(c > 2, c - 3, c)
        return remote(
            eo.at[c, row], er.at[0, k, h, row], eo_s.at[c, side], eo_r.at[k, side, h],
            {"stream": s - h + owner, "span": q},
        )

    def own_edge_in(k, side, st):
        row = pl.ds(1 - side, 1)
        return remote(eo.at[k, row], er.at[0, k, st, row], eo_s.at[k, side], eo_r.at[k, side, st], partner)

    def edge(k, side):
        row = pl.ds(1 - side, 1)
        q = (p_right, p_left)[side]
        return remote(
            es.at[k, :, row], er.at[1, k, :, row], e_s.at[k, side], e_r.at[k, side],
            {"stream": s - h + side_of(k, q), "span": q},
        )

    sent = pl.ds(0, cap)

    def face(f, k, j):
        return remote(
            ys.at[f, k, j, sent], yr.at[f, k, p, sent], i_s.at[f, k], i_r.at[f, k],
            {"stream": s_face + side_of(k, j), "span": j},
        )

    def face_all(f, k):
        return remote(ys.at[f, k, :, sent], yr.at[f, k, :, sent], i_s.at[f, k], i_r.at[f, k], partner)

    local_rs.start()
    local_ck.start()
    local_adj.start()
    local_li.start()

    barrier = pltpu.get_barrier_semaphore()

    def greet(semaphore, stream, span):
        device = {"stream": stream, "span": span}
        pl.semaphore_signal(semaphore, inc=1, device_id=device, device_id_type=MESH)

    def greet_face(semaphore):
        @pl.loop(0, n_span)
        def _(j):
            greet(semaphore, s_face + h, j)

        @pl.when(slots == 3)
        def _():
            @pl.loop(0, n_span // 2)
            def _(j):
                greet(semaphore, s_face + 1 - h, 2 * j + 1 - h)

    greet(barrier, s_pair, p)
    for stream in (s, s_pair):
        greet(barrier, stream, p_left)
        greet(barrier, stream, p_right)

    @pl.when(send_up)
    def _():
        greet(barrier, above["stream"], p)

    @pl.when(up_iface)
    def _():
        greet_face(barrier)

    met = n_span + (slots - 2) * (n_span // 2)


    zero = jnp.zeros((NL, CP), F32)

    @pl.when(jnp.logical_not(has_down))
    def _():
        for f in range(2):
            for k in range(3):
                fld[f, 0, k] = zero

    @pl.when(jnp.logical_not(has_up))
    def _():
        for f in range(2):
            for k in range(3):
                fld[f, 3, k] = zero

    local_rs.wait()

    @pl.when(iface)
    def _():
        rows = rs.shape[0]
        source = rs[...]
        ids = lax.broadcasted_iota(I32, (rows, CP), 0) * CP + lax.broadcasted_iota(I32, (rows, CP), 1)
        rotor = jnp.broadcast_to(count(up_iface), (rows, CP)) == 1
        own = jnp.where(rotor, source, ids)
        far = jnp.where(rotor, ids, source)
        local = div_rows(own) == p
        order = jnp.where(rotor, div_rows(far) * NL + own - p * NL, far)
        order = jnp.where(local, order, 1 << 20)
        row = lax.broadcasted_iota(I32, (NL, CP), 0)
        total = jnp.zeros((NL, CP), I32)
        for i in range(rows):
            total = total + jnp.where(own[i:i + 1, :] == row + p * NL, far[i:i + 1, :], 0)
        link = jnp.sum(total.astype(F32), axis=1, keepdims=True).astype(I32)
        rotor_col = jnp.broadcast_to(count(up_iface), (NL, 1)) == 1
        row_col = lax.broadcasted_iota(I32, (NL, 1), 0)
        key = jnp.where(rotor_col, div_rows(link) * NL + row_col, link)
        keys = jnp.broadcast_to(key, (NL, CP))
        total = jnp.zeros((NL, CP), I32)
        for i in range(rows):
            total = total + jnp.where(order[i:i + 1, :] < keys, 1, 0)
        place = jnp.sum(total.astype(F32), axis=1, keepdims=True).astype(I32)
        place = place + (pad - cap) * div_rows(link)
        lanes = lax.broadcasted_iota(I32, tm.shape, 1)
        tm[...] = jnp.where(jnp.broadcast_to(place, tm.shape) == lanes, 1.0, 0.0).astype(BF16)
        same = lax.broadcasted_iota(I32, (NL, NL), 0) == lax.broadcasted_iota(I32, (NL, NL), 1)
        tmt[...] = dot(tm[...], jnp.where(same, 1.0, 0.0).astype(BF16), ((0,), (0,))).astype(BF16)

    pl.semaphore_wait(barrier, 5 + jnp.where(down_iface, met, count(send_down)))

    @pl.loop(0, other_slots)
    def _(k):
        send_ck(k).start()

    @pl.when(send_down)
    def _():
        greet(ready, below["stream"], p)

    @pl.when(down_iface)
    def _():
        greet_face(ready)

    sel_row = lax.broadcasted_iota(I32, (16, CP), 0)
    sel_lane = lax.broadcasted_iota(I32, (16, CP), 1)
    first, last = sel_lane == 0, sel_lane == CP - 1
    take = jnp.logical_or(jnp.logical_and(sel_row == 0, first), jnp.logical_and(sel_row == 1, last))
    take = jnp.where(take, 1.0, 0.0).astype(BF16)
    give = jnp.where(sel_row < 2, jnp.where(first, 1.0, 0.0), jnp.where(last, 1.0, 0.0))
    give = jnp.where(sel_row < 4, give, 0.0).astype(BF16)

    def edges_of(x):
        hi, lo = split(x)
        return dot(jnp.concatenate([take, take], axis=1), jnp.concatenate([hi, lo], axis=1), ((1,), (1,)))[0:8]

    def scatter_rows(x):
        hi, lo = split(x)
        t = tmt[...]
        y = dot(t, jnp.concatenate([hi, lo], axis=1), ((1,), (0,)))
        return (y[:, :CP] + y[:, CP:]).reshape(n_span, pad, CP)

    local_ck.wait()

    @pl.loop(0, NC)
    def _(c):
        fo[c] = jnp.tanh(cx[c])

    early_up = jnp.logical_and(send_up, h == 1)

    @pl.when(early_up)
    def _():
        pl.semaphore_wait(ready, 1)

    @pl.loop(0, slots)
    def _(k):
        fld[0, h + 1, k] = fo[mine(k)]

        @pl.when(early_up)
        def _():
            field_up(0, k).start()

        @pl.when(jnp.logical_and(send_down, h == 0))
        def _():
            field_down(0, k).start()

    @pl.loop(0, NC)
    def _(c):
        eo[c] = edges_of(fo[c])
        own_edge(c, 0).start()
        own_edge(c, 1).start()

    def send_face(f, k, st):
        ys[f, k] = scatter_rows(fld[f, st + 1, k])

        for j in range(n_span):
            face(f, k, j).start()

    local_adj.wait()
    local_li.wait()
    for b in range(NB):
        rhs = jnp.concatenate([adj[c, b * LB:(b + 1) * LB, :] for c in range(NC)], axis=0).astype(BF16)
        carried = dot(li[b], rhs, ((0,), (0,)))
        for e in range(NC):
            cb[e, b * LB:(b + 1) * LB, :] = carried[e * LB:(e + 1) * LB, :]

    def receive_field(f, k):
        for side in range(2):
            if f == 0:
                own_edge_in(k, side, 0).wait_recv()
                own_edge_in(k, side, 1).wait_recv()
            else:
                edge(k, side).wait_recv()
        r = lax.broadcasted_iota(I32, (16, NL), 0)
        for st in range(2):
            from_left = jnp.broadcast_to(er[f, k, st, 1:2, :], r.shape)
            from_right = jnp.broadcast_to(er[f, k, st, 0:1, :], r.shape)
            v = jnp.where(r < 2, from_left, from_right)
            hi = v.astype(BF16).astype(F32)
            v = jnp.where(lax.rem(r, 2) == 0, hi, v - hi)
            v = jnp.where(r < 4, v, 0.0).astype(BF16)
            hb[st] = dot(v, give, ((0,), (0,)))

        @pl.when(iface)
        def _():
            face_all(f, k).wait_recv()
            held = jnp.where(lax.broadcasted_iota(I32, (n_span, pad, CP), 1) < cap, yr[f, k], 0.0)
            hi, lo = split(held.reshape(n_span * pad, CP))
            t = tm[...]
            y = dot(t, jnp.concatenate([hi, lo], axis=1), ((1,), (0,)))
            fld[f, 3 * count(up_iface), k] = y[:, :CP] + y[:, CP:]

        @pl.when(send_down)
        def _():
            field_up(f, k).wait_recv()

        @pl.when(send_up)
        def _():
            field_down(f, k).wait_recv()

    lane = lax.broadcasted_iota(I32, (HALF, CP), 1)

    def stencil(f, st, k, r, coef_down, coef_up, center, lateral):
        x = fld[f, st + 1, k, r]
        up = fld[f, st, k, r]
        down = fld[f, st + 2, k, r]
        sides = jnp.where(lane == 0, 0.0, pltpu.roll(x, 1, 1)) + jnp.where(lane == CP - 1, 0.0, pltpu.roll(x, CP - 1, 1))
        sides = sides + hb[st, r] - 2.0 * x
        return x, coef_down * down + coef_up * up + center * x + lateral * sides

    def coefs(k):
        c = mine(k)
        advect = pick(ADVECTION, c)
        dissip = pick(DISSIPATION, c)
        return -0.5 * advect + dissip, 0.5 * advect + dissip, -2.0 * dissip, pick(SPREADING, c)

    def flux_step(k):
        send_ck(k).wait_recv()
        fld[0, 2 - h, k] = jnp.tanh(cx[NC + k])

        @pl.when(jnp.logical_and(send_up, h == 0))
        def _():
            field_up(0, k).start()

        @pl.when(jnp.logical_and(send_down, h == 1))
        def _():
            field_down(0, k).start()

        @pl.when(iface)
        def _():
            send_face(0, k, count(up_iface))

    def slope_step(k):
        down_c, up_c, center, lateral = coefs(k)
        receive_field(0, k)

        @pl.loop(0, 2)
        def _(i):
            r = half(i)
            for st in range(2):
                _, op = stencil(0, st, k, r, down_c, up_c, center, lateral)
                t = jnp.tanh(cx[at(st, k), r] + time_step * op)
                fld[1, st + 1, k, r] = 2.0 - t * t

    def weight_step(k):
        send_ca(k).wait_recv()
        for st in range(2):
            fld[1, st + 1, k] = fld[1, st + 1, k] * cb[at(st, k)]

        @pl.when(send_up)
        def _():
            field_up(1, k).start()

        @pl.when(send_down)
        def _():
            field_down(1, k).start()

        @pl.when(iface)
        def _():
            send_face(1, k, count(up_iface))

        for st in range(2):
            es[k, st] = edges_of(fld[1, st + 1, k])
        edge(k, 0).start()
        edge(k, 1).start()

    def result_step(k):
        down_c, up_c, center, lateral = coefs(k)
        receive_field(1, k)

        def result(st, r):
            w, op = stencil(1, st, k, r, up_c, down_c, center, lateral)
            x = fld[0, st + 1, k, r]
            return w + time_step * (1.0 - x * x) * op

        @pl.loop(0, 2)
        def _(i):
            ob[k, half(i)] = result(1 - h, half(i))

        send_out(k, mine(k)).start()

        @pl.loop(0, 2)
        def _(i):
            o_ref[mine(k), half(i)] = result(h, half(i))

    @pl.when(jnp.logical_and(send_up, h == 0))
    def _():
        pl.semaphore_wait(ready, 1)

    @pl.when(up_iface)
    def _():
        pl.semaphore_wait(ready, met)

    @pl.loop(0, slots)
    def _(t):
        flux_step(t)

        @pl.when(t == 0)
        def _():
            @pl.loop(0, other_slots)
            def _(k):
                send_ca(k).start()

    @pl.loop(0, slots)
    def _(k):
        slope_step(k)
        weight_step(k)

    pl.loop(0, slots)(result_step)

    @pl.loop(0, other_slots)
    def _(k):
        send_ck(k).wait_send()
        send_ca(k).wait_send()
        send_out(k, theirs(k)).wait_recv()

    @pl.loop(0, NC)
    def _(c):
        own_edge(c, 0).wait_send()
        own_edge(c, 1).wait_send()

    @pl.loop(0, slots)
    def _(k):
        send_out(k, mine(k)).wait_send()
        edge(k, 0).wait_send()
        edge(k, 1).wait_send()
        for f in range(2):
            @pl.when(send_up)
            def _():
                field_up(f, k).wait_send()

            @pl.when(send_down)
            def _():
                field_down(f, k).wait_send()

        @pl.when(iface)
        def _():
            face_all(0, k).wait_send()
            face_all(1, k).wait_send()


def solution(mesh):
    n_stream, n_span = mesh.shape["stream"], mesh.shape["span"]

    def local(checkpoint, adjoint, line_inverse, row_source):
        pad = -(-(NL // n_span) // 8) * 8
        dma = pltpu.SemaphoreType.DMA
        shape = (NL, CP)

        def body(*refs):
            kernel(n_stream, n_span, *refs)

        operands = (
            checkpoint.reshape(NC, NL, CP),
            adjoint.reshape(NC, NL, CP),
            line_inverse.reshape(NB, NC * LB, NC * LB),
            row_source.reshape(-1, CP),
        )
        out = pl.pallas_call(
            body,
            out_shape=jax.ShapeDtypeStruct((NC, NL, CP), F32),
            in_specs=[pl.BlockSpec(memory_space=pltpu.HBM)] * 4,
            out_specs=pl.BlockSpec(memory_space=pltpu.VMEM),
            scratch_shapes=[
                pltpu.VMEM((NC + 3,) + shape, F32),
                pltpu.VMEM((NC,) + shape, F32),
                pltpu.VMEM((NB, NC * LB, NC * LB), BF16),
                pltpu.VMEM((row_source.size // CP, CP), I32),
                pltpu.VMEM((NC + 3,) + shape, F32),
                pltpu.VMEM((NC,) + shape, F32),
                pltpu.VMEM((2, 4, 3) + shape, F32),
                pltpu.VMEM((2,) + shape, F32),
                pltpu.VMEM((3,) + shape, F32),
                pltpu.VMEM((NC, 8, NL), F32),
                pltpu.VMEM((3, 2, 8, NL), F32),
                pltpu.VMEM((2, 3, 2, 8, NL), F32),
                pltpu.VMEM((2, 3, n_span, pad, CP), F32),
                pltpu.VMEM((2, 3, n_span, pad, CP), F32),
                pltpu.VMEM((NL, n_span * pad), BF16),
                pltpu.VMEM((n_span * pad, NL), BF16),
                dma((4,)), dma((3,)), dma((3,)), dma((3,)), dma((3,)),
                dma((2, 3, 2)), dma((2, 3, 2)), dma((2, 3)), dma((2, 3)),
                dma((NC, 2)), dma((3, 2, 2)), dma((3, 2)), dma((3, 2)), dma((3,)), dma((3,)),
                pltpu.SemaphoreType.REGULAR,
            ],
            compiler_params=pltpu.CompilerParams(
                collective_id=0, has_side_effects=True, vmem_limit_bytes=48 << 20
            ),
            name="adjoint_step",
        )(
            *(pltpu.with_memory_space_constraint(x, pltpu.HBM) for x in operands)
        )
        return out.reshape(NC, NL, 1, CP)

    return jax.shard_map(
        local,
        mesh=mesh,
        in_specs=(
            P(None, None, "stream", "span"),
            P(None, None, "stream", "span"),
            P("stream", None, None, None),
            P(),
        ),
        out_specs=P(None, None, "stream", "span"),
        check_vma=False,
    )
```

```python
import jax
import jax.numpy as jnp
from jax import lax
from jax.experimental import pallas as pl
from jax.experimental.pallas import tpu as pltpu
from jax.sharding import PartitionSpec as P

time_step = 0.5
ADVECTION = (1.0, 0.6, 0.8, 1.2, 0.7)
DISSIPATION = (0.3, 0.25, 0.35, 0.3, 0.4)
SPREADING = (0.4, 0.3, 0.5, 0.35, 0.45)
MESH = pl.DeviceIdType.MESH
NC, NL, CP, NB, LB = 5, 192, 128, 3, 64
HALF = NL // 2
F32, BF16, I32 = jnp.float32, jnp.bfloat16, jnp.int32


def pick(values, index):
    out = jnp.float32(values[-1])
    for i in range(len(values) - 1):
        out = jnp.where(index == i, jnp.float32(values[i]), out)
    return out


def split(x):
    hi = x.astype(BF16)
    return hi, (x - hi.astype(F32)).astype(BF16)


def dot(a, b, dims):
    return lax.dot_general(a, b, (dims, ((), ())), preferred_element_type=F32)


def div_rows(x):
    return lax.shift_right_logical(x * 5462, 20)


def kernel(
    n_stream, n_span, ck_h, adj_h, li_h, rs_h, o_ref,
    cx, adj, li, rs, cb, fo, fld, hb, ob, eo, es, er, ys, yr, tm, tmt,
    l_sem, ck_s, ck_r, ca_s, ca_r, z_s, z_r, i_s, i_r, eo_s, eo_r, e_s, e_r, o_s, o_r, ready, beside,
):
    s = lax.axis_index("stream")
    p = lax.axis_index("span")
    n_z = n_stream // 2
    zi = n_z // 2 - 1
    cap = NL // n_span
    pad = yr.shape[3]
    h = lax.rem(s, 2)
    z = s // 2
    slots = 3 - lax.rem(h + p, 2)
    other_slots = 5 - slots
    up_iface = z == zi
    down_iface = z == zi + 1
    iface = jnp.logical_or(up_iface, down_iface)
    has_up = z < n_z - 1
    has_down = z > 0
    send_up = jnp.logical_and(has_up, jnp.logical_not(up_iface))
    send_down = jnp.logical_and(has_down, jnp.logical_not(down_iface))
    s_face = 2 * jnp.where(up_iface, z + 1, z - 1)
    p_left = lax.rem(p + n_span - 1, n_span)
    p_right = lax.rem(p + 1, n_span)
    s_pair = s + 1 - 2 * h
    partner = {"stream": s_pair, "span": p}
    above = {"stream": lax.rem(s + 2, n_stream), "span": p}
    below = {"stream": lax.rem(s + n_stream - 2, n_stream), "span": p}

    def count(flag):
        return jnp.where(flag, 1, 0)

    def half(i):
        return pl.ds(pl.multiple_of(i * HALF, HALF), HALF)

    def mine(k):
        return jnp.where(k == 2, 2, 3 * h + k)

    def theirs(k):
        return jnp.where(k == 2, 2, 3 - 3 * h + k)

    def at(st, k):
        return jnp.where(h == st, mine(k), NC + k)

    def side_of(k, q):
        return jnp.where(k == 2, lax.rem(q, 2), h)

    def remote(src, dst, send, recv, device):
        return pltpu.make_async_remote_copy(
            src_ref=src, dst_ref=dst, send_sem=send, recv_sem=recv, device_id=device, device_id_type=MESH
        )

    local_ck = pltpu.make_async_copy(ck_h, cx.at[pl.ds(0, NC)], l_sem.at[0])
    local_adj = pltpu.make_async_copy(adj_h, adj, l_sem.at[1])
    local_li = pltpu.make_async_copy(li_h, li, l_sem.at[2])
    local_rs = pltpu.make_async_copy(rs_h, rs, l_sem.at[3])

    def send_ck(k):
        return remote(ck_h.at[theirs(k)], cx.at[NC + k], ck_s.at[k], ck_r.at[k], partner)

    def send_ca(k):
        return remote(cb.at[theirs(k)], cb.at[NC + k], ca_s.at[k], ca_r.at[k], partner)

    def send_out(k, c, i):
        return remote(ob.at[k, half(i)], o_ref.at[c, half(i)], o_s.at[k, i], o_r.at[k, i], partner)

    def field_up(f, k):
        return remote(fld.at[f, 2, k], fld.at[f, 0, k], z_s.at[f, k, 0], z_r.at[f, k, 0], above)

    def field_down(f, k):
        return remote(fld.at[f, 1, k], fld.at[f, 3, k], z_s.at[f, k, 1], z_r.at[f, k, 1], below)

    def own_edge(c, side):
        q = (p_right, p_left)[side]
        row = pl.ds(1 - side, 1)
        owner = jnp.where(c == 2, lax.rem(q, 2), c // 3)
        k = jnp.where(c > 2, c - 3, c)
        return remote(
            eo.at[c, row], er.at[0, k, h, row], eo_s.at[c, side], eo_r.at[k, side, h],
            {"stream": s - h + owner, "span": q},
        )

    def own_edge_in(k, side, st):
        row = pl.ds(1 - side, 1)
        return remote(eo.at[k, row], er.at[0, k, st, row], eo_s.at[k, side], eo_r.at[k, side, st], partner)

    def edge(k, side):
        row = pl.ds(1 - side, 1)
        q = (p_right, p_left)[side]
        return remote(
            es.at[k, :, row], er.at[1, k, :, row], e_s.at[k, side], e_r.at[k, side],
            {"stream": s - h + side_of(k, q), "span": q},
        )

    sent = pl.ds(0, cap)

    def face(f, k, j):
        return remote(
            ys.at[f, k, j, sent], yr.at[f, k, p, sent], i_s.at[f, k], i_r.at[f, k],
            {"stream": s_face + side_of(k, j), "span": j},
        )

    def face_all(f, k):
        return remote(ys.at[f, k, :, sent], yr.at[f, k, :, sent], i_s.at[f, k], i_r.at[f, k], partner)

    local_rs.start()
    local_ck.start()
    local_adj.start()
    local_li.start()

    barrier = pltpu.get_barrier_semaphore()

    def greet(semaphore, stream, span):
        device = {"stream": stream, "span": span}
        pl.semaphore_signal(semaphore, inc=1, device_id=device, device_id_type=MESH)

    def greet_face(semaphore):
        @pl.loop(0, n_span)
        def _(j):
            greet(semaphore, s_face + h, j)

        @pl.when(slots == 3)
        def _():
            @pl.loop(0, n_span // 2)
            def _(j):
                greet(semaphore, s_face + 1 - h, 2 * j + 1 - h)

    def greet_tile(semaphore, q):
        greet(semaphore, s, q)
        greet(semaphore, s_pair, q)

    first_tile = p == 0
    last_tile = p == n_span - 1
    greet(barrier, s_pair, p)

    @pl.when(jnp.logical_not(last_tile))
    def _():
        greet_tile(barrier, p_right)

    @pl.when(first_tile)
    def _():
        greet_tile(barrier, p_left)

    @pl.when(send_up)
    def _():
        greet(barrier, above["stream"], p)

    @pl.when(up_iface)
    def _():
        greet_face(barrier)

    met = n_span + (slots - 2) * (n_span // 2)


    zero = jnp.zeros((NL, CP), F32)

    @pl.when(jnp.logical_not(has_down))
    def _():
        for f in range(2):
            for k in range(3):
                fld[f, 0, k] = zero

    @pl.when(jnp.logical_not(has_up))
    def _():
        for f in range(2):
            for k in range(3):
                fld[f, 3, k] = zero

    sel_row = lax.broadcasted_iota(I32, (16, CP), 0)
    sel_lane = lax.broadcasted_iota(I32, (16, CP), 1)
    first, last = sel_lane == 0, sel_lane == CP - 1
    take = jnp.logical_or(jnp.logical_and(sel_row == 0, first), jnp.logical_and(sel_row == 1, last))
    take = jnp.where(take, 1.0, 0.0).astype(BF16)
    give = jnp.where(sel_row < 2, jnp.where(first, 1.0, 0.0), jnp.where(last, 1.0, 0.0))
    give = jnp.where(sel_row < 4, give, 0.0).astype(BF16)

    def edges_of(x):
        hi, lo = split(x)
        return dot(jnp.concatenate([take, take], axis=1), jnp.concatenate([hi, lo], axis=1), ((1,), (1,)))[0:8]

    def scatter_rows(x):
        hi, lo = split(x)
        t = tmt[...]
        y = dot(t, jnp.concatenate([hi, lo], axis=1), ((1,), (0,)))
        return (y[:, :CP] + y[:, CP:]).reshape(n_span, pad, CP)

    lower = jnp.where(first_tile, 0, jnp.where(last_tile, 4, 2))
    pl.semaphore_wait(barrier, 1 + lower + jnp.where(down_iface, met, count(send_down)))

    @pl.when(send_down)
    def _():
        greet(ready, below["stream"], p)

    send_ck(0).start()
    send_ck(1).start()

    @pl.when(down_iface)
    def _():
        greet_face(ready)

    @pl.when(jnp.logical_not(first_tile))
    def _():
        greet_tile(beside, p_left)

    @pl.when(last_tile)
    def _():
        greet_tile(beside, p_right)

    @pl.when(other_slots == 3)
    def _():
        send_ck(2).start()

    local_ck.wait()

    @pl.loop(0, NC)
    def _(c):
        fo[c] = jnp.tanh(cx[c])

    @pl.loop(0, NC)
    def _(c):
        eo[c] = edges_of(fo[c])

    local_rs.wait()

    @pl.when(iface)
    def _():
        rows = rs.shape[0]
        source = rs[...]
        ids = lax.broadcasted_iota(I32, (rows, CP), 0) * CP + lax.broadcasted_iota(I32, (rows, CP), 1)
        rotor = jnp.broadcast_to(count(up_iface), (rows, CP)) == 1
        own = jnp.where(rotor, source, ids)
        far = jnp.where(rotor, ids, source)
        local = div_rows(own) == p
        order = jnp.where(rotor, div_rows(far) * NL + own - p * NL, far)
        order = jnp.where(local, order, 1 << 20)
        row = lax.broadcasted_iota(I32, (NL, CP), 0)
        total = jnp.zeros((NL, CP), I32)
        for i in range(rows):
            total = total + jnp.where(own[i:i + 1, :] == row + p * NL, far[i:i + 1, :], 0)
        link = jnp.sum(total.astype(F32), axis=1, keepdims=True).astype(I32)
        rotor_col = jnp.broadcast_to(count(up_iface), (NL, 1)) == 1
        row_col = lax.broadcasted_iota(I32, (NL, 1), 0)
        key = jnp.where(rotor_col, div_rows(link) * NL + row_col, link)
        keys = jnp.broadcast_to(key, (NL, CP))
        total = jnp.zeros((NL, CP), I32)
        for i in range(rows):
            total = total + jnp.where(order[i:i + 1, :] < keys, 1, 0)
        place = jnp.sum(total.astype(F32), axis=1, keepdims=True).astype(I32)
        place = place + (pad - cap) * div_rows(link)
        lanes = lax.broadcasted_iota(I32, tm.shape, 1)
        tm[...] = jnp.where(jnp.broadcast_to(place, tm.shape) == lanes, 1.0, 0.0).astype(BF16)
        same = lax.broadcasted_iota(I32, (NL, NL), 0) == lax.broadcasted_iota(I32, (NL, NL), 1)
        tmt[...] = dot(tm[...], jnp.where(same, 1.0, 0.0).astype(BF16), ((0,), (0,))).astype(BF16)

    @pl.loop(0, slots)
    def _(k):
        fld[0, h + 1, k] = fo[mine(k)]

        @pl.when(jnp.logical_and(send_down, h == 0))
        def _():
            field_down(0, k).start()

    def send_face(f, k, st):
        ys[f, k] = scatter_rows(fld[f, st + 1, k])

        for j in range(n_span):
            face(f, k, j).start()

    local_adj.wait()
    local_li.wait()
    for b in range(NB):
        rhs = jnp.concatenate([adj[c, b * LB:(b + 1) * LB, :] for c in range(NC)], axis=0).astype(BF16)
        carried = dot(li[b], rhs, ((0,), (0,)))
        for e in range(NC):
            cb[e, b * LB:(b + 1) * LB, :] = carried[e * LB:(e + 1) * LB, :]

    @pl.when(jnp.logical_not(last_tile))
    def _():
        pl.semaphore_wait(beside, jnp.where(first_tile, 4, 2))

    @pl.loop(0, NC)
    def _(c):
        own_edge(c, 0).start()
        own_edge(c, 1).start()

    def receive_field(f, k):
        for side in range(2):
            if f == 0:
                own_edge_in(k, side, 0).wait_recv()
                own_edge_in(k, side, 1).wait_recv()
            else:
                edge(k, side).wait_recv()
        r = lax.broadcasted_iota(I32, (16, NL), 0)
        for st in range(2):
            from_left = jnp.broadcast_to(er[f, k, st, 1:2, :], r.shape)
            from_right = jnp.broadcast_to(er[f, k, st, 0:1, :], r.shape)
            v = jnp.where(r < 2, from_left, from_right)
            hi = v.astype(BF16).astype(F32)
            v = jnp.where(lax.rem(r, 2) == 0, hi, v - hi)
            v = jnp.where(r < 4, v, 0.0).astype(BF16)
            hb[st] = dot(v, give, ((0,), (0,)))

        @pl.when(iface)
        def _():
            face_all(f, k).wait_recv()
            held = jnp.where(lax.broadcasted_iota(I32, (n_span, pad, CP), 1) < cap, yr[f, k], 0.0)
            hi, lo = split(held.reshape(n_span * pad, CP))
            t = tm[...]
            y = dot(t, jnp.concatenate([hi, lo], axis=1), ((1,), (0,)))
            fld[f, 3 * count(up_iface), k] = y[:, :CP] + y[:, CP:]

        @pl.when(send_down)
        def _():
            field_up(f, k).wait_recv()

        @pl.when(send_up)
        def _():
            field_down(f, k).wait_recv()

    lane = lax.broadcasted_iota(I32, (HALF, CP), 1)

    def stencil(f, st, k, r, coef_down, coef_up, center, lateral):
        x = fld[f, st + 1, k, r]
        up = fld[f, st, k, r]
        down = fld[f, st + 2, k, r]
        sides = jnp.where(lane == 0, 0.0, pltpu.roll(x, 1, 1)) + jnp.where(lane == CP - 1, 0.0, pltpu.roll(x, CP - 1, 1))
        sides = sides + hb[st, r] - 2.0 * x
        return x, coef_down * down + coef_up * up + center * x + lateral * sides

    def coefs(k):
        c = mine(k)
        advect = pick(ADVECTION, c)
        dissip = pick(DISSIPATION, c)
        return -0.5 * advect + dissip, 0.5 * advect + dissip, -2.0 * dissip, pick(SPREADING, c)

    def flux_step(k):
        send_ck(k).wait_recv()
        fld[0, 2 - h, k] = jnp.tanh(cx[NC + k])

        @pl.when(jnp.logical_and(send_down, h == 1))
        def _():
            field_down(0, k).start()

        @pl.when(jnp.logical_and(send_up, h == 0))
        def _():
            @pl.when(k == 0)
            def _():
                pl.semaphore_wait(ready, 1)

            field_up(0, k).start()

        @pl.when(iface)
        def _():
            @pl.when(jnp.logical_and(up_iface, k == 0))
            def _():
                pl.semaphore_wait(ready, met)

            send_face(0, k, count(up_iface))

    def slope_step(k):
        down_c, up_c, center, lateral = coefs(k)
        receive_field(0, k)

        @pl.loop(0, 2)
        def _(i):
            r = half(i)
            for st in range(2):
                _, op = stencil(0, st, k, r, down_c, up_c, center, lateral)
                t = jnp.tanh(cx[at(st, k), r] + time_step * op)
                fld[1, st + 1, k, r] = 2.0 - t * t

    def weight_step(k):
        send_ca(k).wait_recv()
        for st in range(2):
            fld[1, st + 1, k] = fld[1, st + 1, k] * cb[at(st, k)]

        @pl.when(send_up)
        def _():
            field_up(1, k).start()

        @pl.when(send_down)
        def _():
            field_down(1, k).start()

        @pl.when(iface)
        def _():
            send_face(1, k, count(up_iface))

        for st in range(2):
            es[k, st] = edges_of(fld[1, st + 1, k])
        edge(k, 0).start()
        edge(k, 1).start()

    def result_step(k):
        down_c, up_c, center, lateral = coefs(k)
        receive_field(1, k)

        def result(st, r):
            w, op = stencil(1, st, k, r, up_c, down_c, center, lateral)
            x = fld[0, st + 1, k, r]
            return w + time_step * (1.0 - x * x) * op

        @pl.loop(0, 2)
        def _(i):
            ob[k, half(i)] = result(1 - h, half(i))
            send_out(k, mine(k), i).start()

        @pl.loop(0, 2)
        def _(i):
            o_ref[mine(k), half(i)] = result(h, half(i))

    @pl.when(jnp.logical_and(send_up, h == 1))
    def _():
        pl.semaphore_wait(ready, 1)

        @pl.loop(0, slots)
        def _(k):
            field_up(0, k).start()

    @pl.loop(0, slots)
    def _(t):
        flux_step(t)

        @pl.when(t == count(jnp.logical_and(iface, h == 1)) * (slots - 2))
        def _():
            @pl.loop(0, other_slots)
            def _(k):
                send_ca(k).start()

    @pl.loop(0, slots)
    def _(k):
        slope_step(k)
        weight_step(k)

    pl.loop(0, slots)(result_step)

    @pl.loop(0, other_slots)
    def _(k):
        send_ck(k).wait_send()
        send_ca(k).wait_send()
        send_out(k, theirs(k), 0).wait_recv()
        send_out(k, theirs(k), 1).wait_recv()

    @pl.loop(0, NC)
    def _(c):
        own_edge(c, 0).wait_send()
        own_edge(c, 1).wait_send()

    @pl.loop(0, slots)
    def _(k):
        send_out(k, mine(k), 0).wait_send()
        send_out(k, mine(k), 1).wait_send()
        edge(k, 0).wait_send()
        edge(k, 1).wait_send()
        for f in range(2):
            @pl.when(send_up)
            def _():
                field_up(f, k).wait_send()

            @pl.when(send_down)
            def _():
                field_down(f, k).wait_send()

        @pl.when(iface)
        def _():
            face_all(0, k).wait_send()
            face_all(1, k).wait_send()


def solution(mesh):
    n_stream, n_span = mesh.shape["stream"], mesh.shape["span"]

    def local(checkpoint, adjoint, line_inverse, row_source):
        pad = -(-(NL // n_span) // 8) * 8
        dma = pltpu.SemaphoreType.DMA
        shape = (NL, CP)

        def body(*refs):
            kernel(n_stream, n_span, *refs)

        operands = (
            checkpoint.reshape(NC, NL, CP),
            adjoint.reshape(NC, NL, CP),
            line_inverse.reshape(NB, NC * LB, NC * LB),
            row_source.reshape(-1, CP),
        )
        out = pl.pallas_call(
            body,
            out_shape=jax.ShapeDtypeStruct((NC, NL, CP), F32),
            in_specs=[pl.BlockSpec(memory_space=pltpu.HBM)] * 4,
            out_specs=pl.BlockSpec(memory_space=pltpu.VMEM),
            scratch_shapes=[
                pltpu.VMEM((NC + 3,) + shape, F32),
                pltpu.VMEM((NC,) + shape, F32),
                pltpu.VMEM((NB, NC * LB, NC * LB), BF16),
                pltpu.VMEM((row_source.size // CP, CP), I32),
                pltpu.VMEM((NC + 3,) + shape, F32),
                pltpu.VMEM((NC,) + shape, F32),
                pltpu.VMEM((2, 4, 3) + shape, F32),
                pltpu.VMEM((2,) + shape, F32),
                pltpu.VMEM((3,) + shape, F32),
                pltpu.VMEM((NC, 8, NL), F32),
                pltpu.VMEM((3, 2, 8, NL), F32),
                pltpu.VMEM((2, 3, 2, 8, NL), F32),
                pltpu.VMEM((2, 3, n_span, pad, CP), F32),
                pltpu.VMEM((2, 3, n_span, pad, CP), F32),
                pltpu.VMEM((NL, n_span * pad), BF16),
                pltpu.VMEM((n_span * pad, NL), BF16),
                dma((4,)), dma((3,)), dma((3,)), dma((3,)), dma((3,)),
                dma((2, 3, 2)), dma((2, 3, 2)), dma((2, 3)), dma((2, 3)),
                dma((NC, 2)), dma((3, 2, 2)), dma((3, 2)), dma((3, 2)), dma((3, 2)), dma((3, 2)),
                pltpu.SemaphoreType.REGULAR, pltpu.SemaphoreType.REGULAR,
            ],
            compiler_params=pltpu.CompilerParams(
                collective_id=0, has_side_effects=True, vmem_limit_bytes=48 << 20
            ),
            name="adjoint_step",
        )(
            *(pltpu.with_memory_space_constraint(x, pltpu.HBM) for x in operands)
        )
        return out.reshape(NC, NL, 1, CP)

    return jax.shard_map(
        local,
        mesh=mesh,
        in_specs=(
            P(None, None, "stream", "span"),
            P(None, None, "stream", "span"),
            P("stream", None, None, None),
            P(),
        ),
        out_specs=P(None, None, "stream", "span"),
        check_vma=False,
    )
```

```python
import jax
import jax.numpy as jnp
from jax import lax
from jax.experimental import pallas as pl
from jax.experimental.pallas import tpu as pltpu
from jax.sharding import PartitionSpec as P

time_step = 0.5
ADVECTION = (1.0, 0.6, 0.8, 1.2, 0.7)
DISSIPATION = (0.3, 0.25, 0.35, 0.3, 0.4)
SPREADING = (0.4, 0.3, 0.5, 0.35, 0.45)
MESH = pl.DeviceIdType.MESH
NC, NL, CP, NB, LB = 5, 192, 128, 3, 64
HALF = NL // 2
F32, BF16, I32 = jnp.float32, jnp.bfloat16, jnp.int32


def pick(values, index):
    out = jnp.float32(values[-1])
    for i in range(len(values) - 1):
        out = jnp.where(index == i, jnp.float32(values[i]), out)
    return out


def split(x):
    hi = x.astype(BF16)
    return hi, (x - hi.astype(F32)).astype(BF16)


def dot(a, b, dims):
    return lax.dot_general(a, b, (dims, ((), ())), preferred_element_type=F32)


def div_rows(x):
    return lax.shift_right_logical(x * 5462, 20)


def kernel(
    n_stream, n_span, ck_h, adj_h, li_h, rs_h, o_ref,
    cx, adj, li, rs, cb, fo, fld, hb, ob, eo, es, er, ys, yr, tm, tmt,
    l_sem, ck_s, ck_r, ca_s, ca_r, z_s, z_r, i_s, i_r, eo_s, eo_r, e_s, e_r, o_s, o_r, ready, beside,
):
    s = lax.axis_index("stream")
    p = lax.axis_index("span")
    n_z = n_stream // 2
    zi = n_z // 2 - 1
    cap = NL // n_span
    pad = yr.shape[3]
    h = lax.rem(s, 2)
    z = s // 2
    slots = 3 - lax.rem(h + p, 2)
    other_slots = 5 - slots
    up_iface = z == zi
    down_iface = z == zi + 1
    iface = jnp.logical_or(up_iface, down_iface)
    has_up = z < n_z - 1
    has_down = z > 0
    send_up = jnp.logical_and(has_up, jnp.logical_not(up_iface))
    send_down = jnp.logical_and(has_down, jnp.logical_not(down_iface))
    s_face = 2 * jnp.where(up_iface, z + 1, z - 1)
    p_left = lax.rem(p + n_span - 1, n_span)
    p_right = lax.rem(p + 1, n_span)
    s_pair = s + 1 - 2 * h
    partner = {"stream": s_pair, "span": p}
    above = {"stream": lax.rem(s + 2, n_stream), "span": p}
    below = {"stream": lax.rem(s + n_stream - 2, n_stream), "span": p}

    def count(flag):
        return jnp.where(flag, 1, 0)

    def half(i):
        return pl.ds(pl.multiple_of(i * HALF, HALF), HALF)

    def mine(k):
        return jnp.where(k == 2, 2, 3 * h + k)

    def theirs(k):
        return jnp.where(k == 2, 2, 3 - 3 * h + k)

    def at(st, k):
        return jnp.where(h == st, mine(k), NC + k)

    def side_of(k, q):
        return jnp.where(k == 2, lax.rem(q, 2), h)

    def remote(src, dst, send, recv, device):
        return pltpu.make_async_remote_copy(
            src_ref=src, dst_ref=dst, send_sem=send, recv_sem=recv, device_id=device, device_id_type=MESH
        )

    local_ck = pltpu.make_async_copy(ck_h, cx.at[pl.ds(0, NC)], l_sem.at[0])
    local_adj = pltpu.make_async_copy(adj_h, adj, l_sem.at[1])
    local_li = pltpu.make_async_copy(li_h, li, l_sem.at[2])
    local_rs = pltpu.make_async_copy(rs_h, rs, l_sem.at[3])

    def send_ck(k):
        return remote(ck_h.at[theirs(k)], cx.at[NC + k], ck_s.at[k], ck_r.at[k], partner)

    def send_ca(k):
        return remote(cb.at[theirs(k)], cb.at[NC + k], ca_s.at[k], ca_r.at[k], partner)

    def send_out(k, c, i):
        return remote(ob.at[k, half(i)], o_ref.at[c, half(i)], o_s.at[k, i], o_r.at[k, i], partner)

    def field_up(f, k):
        return remote(fld.at[f, 2, k], fld.at[f, 0, k], z_s.at[f, k, 0], z_r.at[f, k, 0], above)

    def field_down(f, k):
        return remote(fld.at[f, 1, k], fld.at[f, 3, k], z_s.at[f, k, 1], z_r.at[f, k, 1], below)

    def own_edge(c, side):
        q = (p_right, p_left)[side]
        row = pl.ds(1 - side, 1)
        owner = jnp.where(c == 2, lax.rem(q, 2), c // 3)
        k = jnp.where(c > 2, c - 3, c)
        return remote(
            eo.at[c, row], er.at[0, k, h, row], eo_s.at[c, side], eo_r.at[k, side, h],
            {"stream": s - h + owner, "span": q},
        )

    def own_edge_in(k, side, st):
        row = pl.ds(1 - side, 1)
        return remote(eo.at[k, row], er.at[0, k, st, row], eo_s.at[k, side], eo_r.at[k, side, st], partner)

    def edge(k, side):
        row = pl.ds(1 - side, 1)
        q = (p_right, p_left)[side]
        return remote(
            es.at[k, :, row], er.at[1, k, :, row], e_s.at[k, side], e_r.at[k, side],
            {"stream": s - h + side_of(k, q), "span": q},
        )

    sent = pl.ds(0, cap)

    def face(f, k, j):
        return remote(
            ys.at[f, k, j, sent], yr.at[f, k, p, sent], i_s.at[f, k], i_r.at[f, k],
            {"stream": s_face + side_of(k, j), "span": j},
        )

    def face_all(f, k):
        return remote(ys.at[f, k, :, sent], yr.at[f, k, :, sent], i_s.at[f, k], i_r.at[f, k], partner)

    barrier = pltpu.get_barrier_semaphore()

    def greet(semaphore, stream, span):
        device = {"stream": stream, "span": span}
        pl.semaphore_signal(semaphore, inc=1, device_id=device, device_id_type=MESH)

    def greet_face(semaphore):
        for j in range(n_span):
            greet(semaphore, s_face + h, j)

        @pl.when(slots == 3)
        def _():
            @pl.loop(0, n_span // 2)
            def _(j):
                greet(semaphore, s_face + 1 - h, 2 * j + 1 - h)

    def greet_tile(semaphore, q):
        greet(semaphore, s, q)
        greet(semaphore, s_pair, q)

    first_tile = p == 0
    last_tile = p == n_span - 1
    greet(barrier, s_pair, p)

    @pl.when(up_iface)
    def _():
        greet_face(barrier)

    @pl.when(jnp.logical_not(last_tile))
    def _():
        greet_tile(barrier, p_right)

    @pl.when(first_tile)
    def _():
        greet_tile(barrier, p_left)

    @pl.when(send_up)
    def _():
        greet(barrier, above["stream"], p)

    met = n_span + (slots - 2) * (n_span // 2)


    local_rs.start()
    local_ck.start()
    local_adj.start()
    local_li.start()

    zero = jnp.zeros((NL, CP), F32)

    @pl.when(jnp.logical_not(has_down))
    def _():
        for f in range(2):
            for k in range(3):
                fld[f, 0, k] = zero

    @pl.when(jnp.logical_not(has_up))
    def _():
        for f in range(2):
            for k in range(3):
                fld[f, 3, k] = zero

    sel_row = lax.broadcasted_iota(I32, (16, CP), 0)
    sel_lane = lax.broadcasted_iota(I32, (16, CP), 1)
    first, last = sel_lane == 0, sel_lane == CP - 1
    take = jnp.logical_or(jnp.logical_and(sel_row == 0, first), jnp.logical_and(sel_row == 1, last))
    take = jnp.where(take, 1.0, 0.0).astype(BF16)
    give = jnp.where(sel_row < 2, jnp.where(first, 1.0, 0.0), jnp.where(last, 1.0, 0.0))
    give = jnp.where(sel_row < 4, give, 0.0).astype(BF16)

    def edges_of(x):
        hi, lo = split(x)
        return dot(jnp.concatenate([take, take], axis=1), jnp.concatenate([hi, lo], axis=1), ((1,), (1,)))[0:8]

    def scatter_rows(x):
        hi, lo = split(x)
        t = tmt[...]
        y = dot(t, jnp.concatenate([hi, lo], axis=1), ((1,), (0,)))
        return (y[:, :CP] + y[:, CP:]).reshape(n_span, pad, CP)

    lower = jnp.where(first_tile, 0, jnp.where(last_tile, 4, 2))
    pl.semaphore_wait(barrier, 1 + lower + jnp.where(down_iface, met, count(send_down)))

    @pl.when(down_iface)
    def _():
        greet_face(ready)

    @pl.when(send_down)
    def _():
        greet(ready, below["stream"], p)

    send_ck(0).start()
    send_ck(1).start()

    @pl.when(jnp.logical_not(first_tile))
    def _():
        greet_tile(beside, p_left)

    @pl.when(last_tile)
    def _():
        greet_tile(beside, p_right)

    @pl.when(other_slots == 3)
    def _():
        send_ck(2).start()

    local_ck.wait()

    @pl.loop(0, NC)
    def _(c):
        fo[c] = jnp.tanh(cx[c])

    @pl.loop(0, NC)
    def _(c):
        eo[c] = edges_of(fo[c])

    local_rs.wait()

    @pl.when(iface)
    def _():
        rows = rs.shape[0]
        source = rs[...]
        ids = lax.broadcasted_iota(I32, (rows, CP), 0) * CP + lax.broadcasted_iota(I32, (rows, CP), 1)
        rotor = jnp.broadcast_to(count(up_iface), (rows, CP)) == 1
        own = jnp.where(rotor, source, ids)
        far = jnp.where(rotor, ids, source)
        local = div_rows(own) == p
        order = jnp.where(rotor, div_rows(far) * NL + own - p * NL, far)
        order = jnp.where(local, order, 1 << 20)
        row = lax.broadcasted_iota(I32, (NL, CP), 0)
        total = jnp.zeros((NL, CP), I32)
        for i in range(rows):
            total = total + jnp.where(own[i:i + 1, :] == row + p * NL, far[i:i + 1, :], 0)
        link = jnp.sum(total.astype(F32), axis=1, keepdims=True).astype(I32)
        rotor_col = jnp.broadcast_to(count(up_iface), (NL, 1)) == 1
        row_col = lax.broadcasted_iota(I32, (NL, 1), 0)
        key = jnp.where(rotor_col, div_rows(link) * NL + row_col, link)
        keys = jnp.broadcast_to(key, (NL, CP))
        total = jnp.zeros((NL, CP), I32)
        for i in range(rows):
            total = total + jnp.where(order[i:i + 1, :] < keys, 1, 0)
        place = jnp.sum(total.astype(F32), axis=1, keepdims=True).astype(I32)
        place = place + (pad - cap) * div_rows(link)
        lanes = lax.broadcasted_iota(I32, tm.shape, 1)
        tm[...] = jnp.where(jnp.broadcast_to(place, tm.shape) == lanes, 1.0, 0.0).astype(BF16)
        same = lax.broadcasted_iota(I32, (NL, NL), 0) == lax.broadcasted_iota(I32, (NL, NL), 1)
        tmt[...] = dot(tm[...], jnp.where(same, 1.0, 0.0).astype(BF16), ((0,), (0,))).astype(BF16)

    @pl.loop(0, slots)
    def _(k):
        fld[0, h + 1, k] = fo[mine(k)]

        @pl.when(jnp.logical_and(send_down, h == 0))
        def _():
            field_down(0, k).start()

    def send_face(f, k, st):
        ys[f, k] = scatter_rows(fld[f, st + 1, k])

        for j in range(n_span):
            face(f, k, j).start()

    local_adj.wait()
    local_li.wait()
    for b in range(NB):
        rhs = jnp.concatenate([adj[c, b * LB:(b + 1) * LB, :] for c in range(NC)], axis=0).astype(BF16)
        carried = dot(li[b], rhs, ((0,), (0,)))
        for e in range(NC):
            cb[e, b * LB:(b + 1) * LB, :] = carried[e * LB:(e + 1) * LB, :]

    @pl.when(jnp.logical_not(last_tile))
    def _():
        pl.semaphore_wait(beside, jnp.where(first_tile, 4, 2))

    @pl.loop(0, NC)
    def _(c):
        own_edge(c, 0).start()
        own_edge(c, 1).start()

    def receive_field(f, k):
        for side in range(2):
            if f == 0:
                own_edge_in(k, side, 0).wait_recv()
                own_edge_in(k, side, 1).wait_recv()
            else:
                edge(k, side).wait_recv()
        r = lax.broadcasted_iota(I32, (16, NL), 0)
        for st in range(2):
            from_left = jnp.broadcast_to(er[f, k, st, 1:2, :], r.shape)
            from_right = jnp.broadcast_to(er[f, k, st, 0:1, :], r.shape)
            v = jnp.where(r < 2, from_left, from_right)
            hi = v.astype(BF16).astype(F32)
            v = jnp.where(lax.rem(r, 2) == 0, hi, v - hi)
            v = jnp.where(r < 4, v, 0.0).astype(BF16)
            hb[st] = dot(v, give, ((0,), (0,)))

        @pl.when(iface)
        def _():
            face_all(f, k).wait_recv()
            held = jnp.where(lax.broadcasted_iota(I32, (n_span, pad, CP), 1) < cap, yr[f, k], 0.0)
            hi, lo = split(held.reshape(n_span * pad, CP))
            t = tm[...]
            y = dot(t, jnp.concatenate([hi, lo], axis=1), ((1,), (0,)))
            fld[f, 3 * count(up_iface), k] = y[:, :CP] + y[:, CP:]

        @pl.when(send_down)
        def _():
            field_up(f, k).wait_recv()

        @pl.when(send_up)
        def _():
            field_down(f, k).wait_recv()

    lane = lax.broadcasted_iota(I32, (HALF, CP), 1)

    def stencil(f, st, k, r, coef_down, coef_up, center, lateral):
        x = fld[f, st + 1, k, r]
        up = fld[f, st, k, r]
        down = fld[f, st + 2, k, r]
        sides = jnp.where(lane == 0, 0.0, pltpu.roll(x, 1, 1)) + jnp.where(lane == CP - 1, 0.0, pltpu.roll(x, CP - 1, 1))
        sides = sides + hb[st, r] - 2.0 * x
        return x, coef_down * down + coef_up * up + center * x + lateral * sides

    def coefs(k):
        c = mine(k)
        advect = pick(ADVECTION, c)
        dissip = pick(DISSIPATION, c)
        return -0.5 * advect + dissip, 0.5 * advect + dissip, -2.0 * dissip, pick(SPREADING, c)

    def flux_step(k):
        send_ck(k).wait_recv()
        fld[0, 2 - h, k] = jnp.tanh(cx[NC + k])

        @pl.when(jnp.logical_and(send_down, h == 1))
        def _():
            field_down(0, k).start()

        @pl.when(jnp.logical_and(send_up, h == 0))
        def _():
            @pl.when(k == 0)
            def _():
                pl.semaphore_wait(ready, 1)

            field_up(0, k).start()

        @pl.when(iface)
        def _():
            @pl.when(jnp.logical_and(up_iface, k == 0))
            def _():
                pl.semaphore_wait(ready, met)

            send_face(0, k, count(up_iface))

    def slope_step(k):
        down_c, up_c, center, lateral = coefs(k)
        receive_field(0, k)

        @pl.loop(0, 2)
        def _(i):
            r = half(i)
            for st in range(2):
                _, op = stencil(0, st, k, r, down_c, up_c, center, lateral)
                t = jnp.tanh(cx[at(st, k), r] + time_step * op)
                fld[1, st + 1, k, r] = 2.0 - t * t

    def weight_step(k):
        send_ca(k).wait_recv()
        for st in range(2):
            fld[1, st + 1, k] = fld[1, st + 1, k] * cb[at(st, k)]

        @pl.when(send_up)
        def _():
            field_up(1, k).start()

        @pl.when(send_down)
        def _():
            field_down(1, k).start()

        @pl.when(iface)
        def _():
            send_face(1, k, count(up_iface))

        for st in range(2):
            es[k, st] = edges_of(fld[1, st + 1, k])
        edge(k, 0).start()
        edge(k, 1).start()

    def result_step(k):
        down_c, up_c, center, lateral = coefs(k)
        receive_field(1, k)

        def result(st, r):
            w, op = stencil(1, st, k, r, up_c, down_c, center, lateral)
            x = fld[0, st + 1, k, r]
            return w + time_step * (1.0 - x * x) * op

        @pl.loop(0, 2)
        def _(i):
            ob[k, half(i)] = result(1 - h, half(i))
            send_out(k, mine(k), i).start()

        @pl.loop(0, 2)
        def _(i):
            o_ref[mine(k), half(i)] = result(h, half(i))

    @pl.when(jnp.logical_and(send_up, h == 1))
    def _():
        pl.semaphore_wait(ready, 1)

        @pl.loop(0, slots)
        def _(k):
            field_up(0, k).start()

    @pl.loop(0, slots)
    def _(t):
        flux_step(t)

        @pl.when(t == count(jnp.logical_and(iface, h == 1)) * (slots - 2))
        def _():
            @pl.loop(0, other_slots)
            def _(k):
                send_ca(k).start()

    @pl.loop(0, slots)
    def _(k):
        slope_step(k)
        weight_step(k)

    pl.loop(0, slots)(result_step)

    @pl.loop(0, other_slots)
    def _(k):
        send_ck(k).wait_send()
        send_ca(k).wait_send()
        send_out(k, theirs(k), 0).wait_recv()
        send_out(k, theirs(k), 1).wait_recv()

    @pl.loop(0, NC)
    def _(c):
        own_edge(c, 0).wait_send()
        own_edge(c, 1).wait_send()

    @pl.loop(0, slots)
    def _(k):
        send_out(k, mine(k), 0).wait_send()
        send_out(k, mine(k), 1).wait_send()
        edge(k, 0).wait_send()
        edge(k, 1).wait_send()
        for f in range(2):
            @pl.when(send_up)
            def _():
                field_up(f, k).wait_send()

            @pl.when(send_down)
            def _():
                field_down(f, k).wait_send()

        @pl.when(iface)
        def _():
            face_all(0, k).wait_send()
            face_all(1, k).wait_send()


def solution(mesh):
    n_stream, n_span = mesh.shape["stream"], mesh.shape["span"]

    def local(checkpoint, adjoint, line_inverse, row_source):
        pad = -(-(NL // n_span) // 8) * 8
        dma = pltpu.SemaphoreType.DMA
        shape = (NL, CP)

        def body(*refs):
            kernel(n_stream, n_span, *refs)

        operands = (
            checkpoint.reshape(NC, NL, CP),
            adjoint.reshape(NC, NL, CP),
            line_inverse.reshape(NB, NC * LB, NC * LB),
            row_source.reshape(-1, CP),
        )
        out = pl.pallas_call(
            body,
            out_shape=jax.ShapeDtypeStruct((NC, NL, CP), F32),
            in_specs=[pl.BlockSpec(memory_space=pltpu.HBM)] * 4,
            out_specs=pl.BlockSpec(memory_space=pltpu.VMEM),
            scratch_shapes=[
                pltpu.VMEM((NC + 3,) + shape, F32),
                pltpu.VMEM((NC,) + shape, F32),
                pltpu.VMEM((NB, NC * LB, NC * LB), BF16),
                pltpu.VMEM((row_source.size // CP, CP), I32),
                pltpu.VMEM((NC + 3,) + shape, F32),
                pltpu.VMEM((NC,) + shape, F32),
                pltpu.VMEM((2, 4, 3) + shape, F32),
                pltpu.VMEM((2,) + shape, F32),
                pltpu.VMEM((3,) + shape, F32),
                pltpu.VMEM((NC, 8, NL), F32),
                pltpu.VMEM((3, 2, 8, NL), F32),
                pltpu.VMEM((2, 3, 2, 8, NL), F32),
                pltpu.VMEM((2, 3, n_span, pad, CP), F32),
                pltpu.VMEM((2, 3, n_span, pad, CP), F32),
                pltpu.VMEM((NL, n_span * pad), BF16),
                pltpu.VMEM((n_span * pad, NL), BF16),
                dma((4,)), dma((3,)), dma((3,)), dma((3,)), dma((3,)),
                dma((2, 3, 2)), dma((2, 3, 2)), dma((2, 3)), dma((2, 3)),
                dma((NC, 2)), dma((3, 2, 2)), dma((3, 2)), dma((3, 2)), dma((3, 2)), dma((3, 2)),
                pltpu.SemaphoreType.REGULAR, pltpu.SemaphoreType.REGULAR,
            ],
            compiler_params=pltpu.CompilerParams(
                collective_id=0, has_side_effects=True, vmem_limit_bytes=48 << 20
            ),
            name="adjoint_step",
        )(
            *(pltpu.with_memory_space_constraint(x, pltpu.HBM) for x in operands)
        )
        return out.reshape(NC, NL, 1, CP)

    return jax.shard_map(
        local,
        mesh=mesh,
        in_specs=(
            P(None, None, "stream", "span"),
            P(None, None, "stream", "span"),
            P("stream", None, None, None),
            P(),
        ),
        out_specs=P(None, None, "stream", "span"),
        check_vma=False,
    )
```

```python
import jax
import jax.numpy as jnp
from jax import lax
from jax.experimental import pallas as pl
from jax.experimental.pallas import tpu as pltpu
from jax.sharding import PartitionSpec as P

time_step = 0.5
ADVECTION = (1.0, 0.6, 0.8, 1.2, 0.7)
DISSIPATION = (0.3, 0.25, 0.35, 0.3, 0.4)
SPREADING = (0.4, 0.3, 0.5, 0.35, 0.45)
MESH = pl.DeviceIdType.MESH
NC, NL, CP, NB, LB = 5, 192, 128, 3, 64
HALF = NL // 2
F32, BF16, I32 = jnp.float32, jnp.bfloat16, jnp.int32


def pick(values, index):
    out = jnp.float32(values[-1])
    for i in range(len(values) - 1):
        out = jnp.where(index == i, jnp.float32(values[i]), out)
    return out


def split(x):
    hi = x.astype(BF16)
    return hi, (x - hi.astype(F32)).astype(BF16)


def dot(a, b, dims):
    return lax.dot_general(a, b, (dims, ((), ())), preferred_element_type=F32)


def div_rows(x):
    return lax.shift_right_logical(x * 5462, 20)


def kernel(
    n_stream, n_span, ck_h, adj_h, li_h, rs_h, o_ref,
    cx, adj, li, rs, cb, fo, fld, hb, ob, eo, es, er, ys, yr, tm, tmt,
    l_sem, ck_s, ck_r, ca_s, ca_r, z_s, z_r, i_s, i_r, eo_s, eo_r, e_s, e_r, o_s, o_r, ready, beside,
):
    s = lax.axis_index("stream")
    p = lax.axis_index("span")
    n_z = n_stream // 2
    zi = n_z // 2 - 1
    cap = NL // n_span
    pad = yr.shape[3]
    h = lax.rem(s, 2)
    z = s // 2
    slots = 3 - lax.rem(h + p, 2)
    other_slots = 5 - slots
    up_iface = z == zi
    down_iface = z == zi + 1
    iface = jnp.logical_or(up_iface, down_iface)
    has_up = z < n_z - 1
    has_down = z > 0
    send_up = jnp.logical_and(has_up, jnp.logical_not(up_iface))
    send_down = jnp.logical_and(has_down, jnp.logical_not(down_iface))
    s_face = 2 * jnp.where(up_iface, z + 1, z - 1)
    p_left = lax.rem(p + n_span - 1, n_span)
    p_right = lax.rem(p + 1, n_span)
    s_pair = s + 1 - 2 * h
    partner = {"stream": s_pair, "span": p}
    above = {"stream": lax.rem(s + 2, n_stream), "span": p}
    below = {"stream": lax.rem(s + n_stream - 2, n_stream), "span": p}

    def count(flag):
        return jnp.where(flag, 1, 0)

    def half(i):
        return pl.ds(pl.multiple_of(i * HALF, HALF), HALF)

    def mine(k):
        return jnp.where(k == 2, 2, 3 * h + k)

    def theirs(k):
        return jnp.where(k == 2, 2, 3 - 3 * h + k)

    def at(st, k):
        return jnp.where(h == st, mine(k), NC + k)

    def side_of(k, q):
        return jnp.where(k == 2, lax.rem(q, 2), h)

    def remote(src, dst, send, recv, device):
        return pltpu.make_async_remote_copy(
            src_ref=src, dst_ref=dst, send_sem=send, recv_sem=recv, device_id=device, device_id_type=MESH
        )

    local_ck = pltpu.make_async_copy(ck_h, cx.at[pl.ds(0, NC)], l_sem.at[0])
    local_adj = pltpu.make_async_copy(adj_h, adj, l_sem.at[1])
    local_li = pltpu.make_async_copy(li_h, li, l_sem.at[2])
    local_rs = pltpu.make_async_copy(rs_h, rs, l_sem.at[3])

    def send_ck(k):
        return remote(ck_h.at[theirs(k)], cx.at[NC + k], ck_s.at[k], ck_r.at[k], partner)

    def send_ca(k):
        return remote(cb.at[theirs(k)], cb.at[NC + k], ca_s.at[k], ca_r.at[k], partner)

    def send_out(k, c, i):
        return remote(ob.at[k, half(i)], o_ref.at[c, half(i)], o_s.at[k, i], o_r.at[k, i], partner)

    def field_up(f, k):
        return remote(fld.at[f, 2, k], fld.at[f, 0, k], z_s.at[f, k, 0], z_r.at[f, k, 0], above)

    def field_down(f, k):
        return remote(fld.at[f, 1, k], fld.at[f, 3, k], z_s.at[f, k, 1], z_r.at[f, k, 1], below)

    def own_edge(c, side):
        q = (p_right, p_left)[side]
        row = pl.ds(1 - side, 1)
        owner = jnp.where(c == 2, lax.rem(q, 2), c // 3)
        k = jnp.where(c > 2, c - 3, c)
        return remote(
            eo.at[c, row], er.at[0, k, h, row], eo_s.at[c, side], eo_r.at[k, side, h],
            {"stream": s - h + owner, "span": q},
        )

    def own_edge_in(k, side, st):
        row = pl.ds(1 - side, 1)
        return remote(eo.at[k, row], er.at[0, k, st, row], eo_s.at[k, side], eo_r.at[k, side, st], partner)

    def edge(k, side, st):
        row = pl.ds(1 - side, 1)
        q = (p_right, p_left)[side]
        return remote(
            es.at[k, st, row], er.at[1, k, st, row], e_s.at[k, side, st], e_r.at[k, side, st],
            {"stream": s - h + side_of(k, q), "span": q},
        )

    sent = pl.ds(0, cap)

    def face(f, k, j):
        return remote(
            ys.at[f, k, j, sent], yr.at[f, k, p, sent], i_s.at[f, k], i_r.at[f, k],
            {"stream": s_face + side_of(k, j), "span": j},
        )

    def face_all(f, k):
        return remote(ys.at[f, k, :, sent], yr.at[f, k, :, sent], i_s.at[f, k], i_r.at[f, k], partner)

    local_rs.start()
    local_ck.start()
    local_adj.start()
    local_li.start()

    barrier = pltpu.get_barrier_semaphore()

    def greet(semaphore, stream, span):
        device = {"stream": stream, "span": span}
        pl.semaphore_signal(semaphore, inc=1, device_id=device, device_id_type=MESH)

    def greet_face(semaphore):
        @pl.loop(0, n_span)
        def _(j):
            greet(semaphore, s_face + h, j)

        @pl.when(slots == 3)
        def _():
            @pl.loop(0, n_span // 2)
            def _(j):
                greet(semaphore, s_face + 1 - h, 2 * j + 1 - h)

    def greet_tile(semaphore, q):
        greet(semaphore, s, q)
        greet(semaphore, s_pair, q)

    first_tile = p == 0
    last_tile = p == n_span - 1
    greet(barrier, s_pair, p)

    @pl.when(jnp.logical_not(last_tile))
    def _():
        greet_tile(barrier, p_right)

    @pl.when(first_tile)
    def _():
        greet_tile(barrier, p_left)

    @pl.when(send_up)
    def _():
        greet(barrier, above["stream"], p)

    @pl.when(up_iface)
    def _():
        greet_face(barrier)

    met = n_span + (slots - 2) * (n_span // 2)


    zero = jnp.zeros((NL, CP), F32)

    @pl.when(jnp.logical_not(has_down))
    def _():
        for f in range(2):
            for k in range(3):
                fld[f, 0, k] = zero

    @pl.when(jnp.logical_not(has_up))
    def _():
        for f in range(2):
            for k in range(3):
                fld[f, 3, k] = zero

    sel_row = lax.broadcasted_iota(I32, (16, CP), 0)
    sel_lane = lax.broadcasted_iota(I32, (16, CP), 1)
    first, last = sel_lane == 0, sel_lane == CP - 1
    take = jnp.logical_or(jnp.logical_and(sel_row == 0, first), jnp.logical_and(sel_row == 1, last))
    take = jnp.where(take, 1.0, 0.0).astype(BF16)
    give = jnp.where(sel_row < 2, jnp.where(first, 1.0, 0.0), jnp.where(last, 1.0, 0.0))
    give = jnp.where(sel_row < 4, give, 0.0).astype(BF16)

    def edges_of(x):
        hi, lo = split(x)
        return dot(jnp.concatenate([take, take], axis=1), jnp.concatenate([hi, lo], axis=1), ((1,), (1,)))[0:8]

    def scatter_rows(x):
        hi, lo = split(x)
        t = tmt[...]
        y = dot(t, jnp.concatenate([hi, lo], axis=1), ((1,), (0,)))
        return (y[:, :CP] + y[:, CP:]).reshape(n_span, pad, CP)

    lower = jnp.where(first_tile, 0, jnp.where(last_tile, 4, 2))
    pl.semaphore_wait(barrier, 1 + lower + jnp.where(down_iface, met, count(send_down)))

    @pl.when(send_down)
    def _():
        greet(ready, below["stream"], p)

    send_ck(0).start()
    send_ck(1).start()

    @pl.when(down_iface)
    def _():
        greet_face(ready)

    @pl.when(jnp.logical_not(first_tile))
    def _():
        greet_tile(beside, p_left)

    @pl.when(last_tile)
    def _():
        greet_tile(beside, p_right)

    @pl.when(other_slots == 3)
    def _():
        send_ck(2).start()

    local_ck.wait()

    @pl.loop(0, NC)
    def _(c):
        fo[c] = jnp.tanh(cx[c])

    @pl.loop(0, NC)
    def _(c):
        eo[c] = edges_of(fo[c])

    local_rs.wait()

    @pl.when(iface)
    def _():
        rows = rs.shape[0]
        source = rs[...]
        ids = lax.broadcasted_iota(I32, (rows, CP), 0) * CP + lax.broadcasted_iota(I32, (rows, CP), 1)
        rotor = jnp.broadcast_to(count(up_iface), (rows, CP)) == 1
        own = jnp.where(rotor, source, ids)
        far = jnp.where(rotor, ids, source)
        local = div_rows(own) == p
        order = jnp.where(rotor, div_rows(far) * NL + own - p * NL, far)
        order = jnp.where(local, order, 1 << 20)
        row = lax.broadcasted_iota(I32, (NL, CP), 0)
        total = jnp.zeros((NL, CP), I32)
        for i in range(rows):
            total = total + jnp.where(own[i:i + 1, :] == row + p * NL, far[i:i + 1, :], 0)
        link = jnp.sum(total.astype(F32), axis=1, keepdims=True).astype(I32)
        rotor_col = jnp.broadcast_to(count(up_iface), (NL, 1)) == 1
        row_col = lax.broadcasted_iota(I32, (NL, 1), 0)
        key = jnp.where(rotor_col, div_rows(link) * NL + row_col, link)
        keys = jnp.broadcast_to(key, (NL, CP))
        total = jnp.zeros((NL, CP), I32)
        for i in range(rows):
            total = total + jnp.where(order[i:i + 1, :] < keys, 1, 0)
        place = jnp.sum(total.astype(F32), axis=1, keepdims=True).astype(I32)
        place = place + (pad - cap) * div_rows(link)
        lanes = lax.broadcasted_iota(I32, tm.shape, 1)
        tm[...] = jnp.where(jnp.broadcast_to(place, tm.shape) == lanes, 1.0, 0.0).astype(BF16)
        same = lax.broadcasted_iota(I32, (NL, NL), 0) == lax.broadcasted_iota(I32, (NL, NL), 1)
        tmt[...] = dot(tm[...], jnp.where(same, 1.0, 0.0).astype(BF16), ((0,), (0,))).astype(BF16)

    @pl.loop(0, slots)
    def _(k):
        fld[0, h + 1, k] = fo[mine(k)]

        @pl.when(jnp.logical_and(send_down, h == 0))
        def _():
            field_down(0, k).start()

    def send_face(f, k, st):
        ys[f, k] = scatter_rows(fld[f, st + 1, k])

        for j in range(n_span):
            face(f, k, j).start()

    local_adj.wait()
    local_li.wait()
    for b in range(NB):
        rhs = jnp.concatenate([adj[c, b * LB:(b + 1) * LB, :] for c in range(NC)], axis=0).astype(BF16)
        carried = dot(li[b], rhs, ((0,), (0,)))
        for e in range(NC):
            cb[e, b * LB:(b + 1) * LB, :] = carried[e * LB:(e + 1) * LB, :]

    @pl.when(jnp.logical_not(last_tile))
    def _():
        pl.semaphore_wait(beside, jnp.where(first_tile, 4, 2))

    @pl.loop(0, NC)
    def _(c):
        own_edge(c, 0).start()
        own_edge(c, 1).start()

    def receive_field(f, k):
        for side in range(2):
            for st in range(2):
                message = edge(k, side, st) if f else own_edge_in(k, side, st)
                message.wait_recv()
        r = lax.broadcasted_iota(I32, (16, NL), 0)
        for st in range(2):
            from_left = jnp.broadcast_to(er[f, k, st, 1:2, :], r.shape)
            from_right = jnp.broadcast_to(er[f, k, st, 0:1, :], r.shape)
            v = jnp.where(r < 2, from_left, from_right)
            hi = v.astype(BF16).astype(F32)
            v = jnp.where(lax.rem(r, 2) == 0, hi, v - hi)
            v = jnp.where(r < 4, v, 0.0).astype(BF16)
            hb[st] = dot(v, give, ((0,), (0,)))

        @pl.when(iface)
        def _():
            face_all(f, k).wait_recv()
            held = jnp.where(lax.broadcasted_iota(I32, (n_span, pad, CP), 1) < cap, yr[f, k], 0.0)
            hi, lo = split(held.reshape(n_span * pad, CP))
            t = tm[...]
            y = dot(t, jnp.concatenate([hi, lo], axis=1), ((1,), (0,)))
            fld[f, 3 * count(up_iface), k] = y[:, :CP] + y[:, CP:]

        @pl.when(send_down)
        def _():
            field_up(f, k).wait_recv()

        @pl.when(send_up)
        def _():
            field_down(f, k).wait_recv()

    lane = lax.broadcasted_iota(I32, (HALF, CP), 1)

    def stencil(f, st, k, r, coef_down, coef_up, center, lateral):
        x = fld[f, st + 1, k, r]
        up = fld[f, st, k, r]
        down = fld[f, st + 2, k, r]
        sides = jnp.where(lane == 0, 0.0, pltpu.roll(x, 1, 1)) + jnp.where(lane == CP - 1, 0.0, pltpu.roll(x, CP - 1, 1))
        sides = sides + hb[st, r] - 2.0 * x
        return x, coef_down * down + coef_up * up + center * x + lateral * sides

    def coefs(k):
        c = mine(k)
        advect = pick(ADVECTION, c)
        dissip = pick(DISSIPATION, c)
        return -0.5 * advect + dissip, 0.5 * advect + dissip, -2.0 * dissip, pick(SPREADING, c)

    def flux_step(k):
        send_ck(k).wait_recv()
        fld[0, 2 - h, k] = jnp.tanh(cx[NC + k])

        @pl.when(jnp.logical_and(send_down, h == 1))
        def _():
            field_down(0, k).start()

        @pl.when(jnp.logical_and(send_up, h == 0))
        def _():
            @pl.when(k == 0)
            def _():
                pl.semaphore_wait(ready, 1)

            field_up(0, k).start()

        @pl.when(iface)
        def _():
            @pl.when(jnp.logical_and(up_iface, k == 0))
            def _():
                pl.semaphore_wait(ready, met)

            send_face(0, k, count(up_iface))

    def slope_step(k):
        down_c, up_c, center, lateral = coefs(k)
        receive_field(0, k)

        @pl.loop(0, 2)
        def _(i):
            r = half(i)
            for st in range(2):
                _, op = stencil(0, st, k, r, down_c, up_c, center, lateral)
                t = jnp.tanh(cx[at(st, k), r] + time_step * op)
                fld[1, st + 1, k, r] = 2.0 - t * t

    def weight_step(k, st):
        fld[1, st + 1, k] = fld[1, st + 1, k] * cb[at(st, k)]

        @pl.when(jnp.logical_and(send_up, st == 1))
        def _():
            field_up(1, k).start()

        @pl.when(jnp.logical_and(send_down, st == 0))
        def _():
            field_down(1, k).start()

        @pl.when(jnp.logical_and(iface, st == count(up_iface)))
        def _():
            send_face(1, k, st)

        es[k, st] = edges_of(fld[1, st + 1, k])
        edge(k, 0, st).start()
        edge(k, 1, st).start()

    def far_step(k):
        send_ca(k).wait_recv()
        weight_step(k, 1 - h)

    def result_step(k):
        down_c, up_c, center, lateral = coefs(k)
        receive_field(1, k)

        def result(st, r):
            w, op = stencil(1, st, k, r, up_c, down_c, center, lateral)
            x = fld[0, st + 1, k, r]
            return w + time_step * (1.0 - x * x) * op

        @pl.loop(0, 2)
        def _(i):
            ob[k, half(i)] = result(1 - h, half(i))
            send_out(k, mine(k), i).start()

        @pl.loop(0, 2)
        def _(i):
            o_ref[mine(k), half(i)] = result(h, half(i))

    @pl.when(jnp.logical_and(send_up, h == 1))
    def _():
        pl.semaphore_wait(ready, 1)

        @pl.loop(0, slots)
        def _(k):
            field_up(0, k).start()

    @pl.loop(0, slots)
    def _(t):
        flux_step(t)

        @pl.when(t == count(jnp.logical_and(iface, h == 1)) * (slots - 2))
        def _():
            @pl.loop(0, other_slots)
            def _(k):
                send_ca(k).start()

    @pl.loop(0, slots)
    def _(k):
        slope_step(k)
        weight_step(k, h)
        far_step(k)

    pl.loop(0, slots)(result_step)

    @pl.loop(0, other_slots)
    def _(k):
        send_ck(k).wait_send()
        send_ca(k).wait_send()
        send_out(k, theirs(k), 0).wait_recv()
        send_out(k, theirs(k), 1).wait_recv()

    @pl.loop(0, NC)
    def _(c):
        own_edge(c, 0).wait_send()
        own_edge(c, 1).wait_send()

    @pl.loop(0, slots)
    def _(k):
        send_out(k, mine(k), 0).wait_send()
        send_out(k, mine(k), 1).wait_send()
        for side in range(2):
            for st in range(2):
                edge(k, side, st).wait_send()
        for f in range(2):
            @pl.when(send_up)
            def _():
                field_up(f, k).wait_send()

            @pl.when(send_down)
            def _():
                field_down(f, k).wait_send()

        @pl.when(iface)
        def _():
            face_all(0, k).wait_send()
            face_all(1, k).wait_send()


def solution(mesh):
    n_stream, n_span = mesh.shape["stream"], mesh.shape["span"]

    def local(checkpoint, adjoint, line_inverse, row_source):
        pad = -(-(NL // n_span) // 8) * 8
        dma = pltpu.SemaphoreType.DMA
        shape = (NL, CP)

        def body(*refs):
            kernel(n_stream, n_span, *refs)

        operands = (
            checkpoint.reshape(NC, NL, CP),
            adjoint.reshape(NC, NL, CP),
            line_inverse.reshape(NB, NC * LB, NC * LB),
            row_source.reshape(-1, CP),
        )
        out = pl.pallas_call(
            body,
            out_shape=jax.ShapeDtypeStruct((NC, NL, CP), F32),
            in_specs=[pl.BlockSpec(memory_space=pltpu.HBM)] * 4,
            out_specs=pl.BlockSpec(memory_space=pltpu.VMEM),
            scratch_shapes=[
                pltpu.VMEM((NC + 3,) + shape, F32),
                pltpu.VMEM((NC,) + shape, F32),
                pltpu.VMEM((NB, NC * LB, NC * LB), BF16),
                pltpu.VMEM((row_source.size // CP, CP), I32),
                pltpu.VMEM((NC + 3,) + shape, F32),
                pltpu.VMEM((NC,) + shape, F32),
                pltpu.VMEM((2, 4, 3) + shape, F32),
                pltpu.VMEM((2,) + shape, F32),
                pltpu.VMEM((3,) + shape, F32),
                pltpu.VMEM((NC, 8, NL), F32),
                pltpu.VMEM((3, 2, 8, NL), F32),
                pltpu.VMEM((2, 3, 2, 8, NL), F32),
                pltpu.VMEM((2, 3, n_span, pad, CP), F32),
                pltpu.VMEM((2, 3, n_span, pad, CP), F32),
                pltpu.VMEM((NL, n_span * pad), BF16),
                pltpu.VMEM((n_span * pad, NL), BF16),
                dma((4,)), dma((3,)), dma((3,)), dma((3,)), dma((3,)),
                dma((2, 3, 2)), dma((2, 3, 2)), dma((2, 3)), dma((2, 3)),
                dma((NC, 2)), dma((3, 2, 2)), dma((3, 2, 2)), dma((3, 2, 2)), dma((3, 2)), dma((3, 2)),
                pltpu.SemaphoreType.REGULAR, pltpu.SemaphoreType.REGULAR,
            ],
            compiler_params=pltpu.CompilerParams(
                collective_id=0, has_side_effects=True, vmem_limit_bytes=48 << 20
            ),
            name="adjoint_step",
        )(
            *(pltpu.with_memory_space_constraint(x, pltpu.HBM) for x in operands)
        )
        return out.reshape(NC, NL, 1, CP)

    return jax.shard_map(
        local,
        mesh=mesh,
        in_specs=(
            P(None, None, "stream", "span"),
            P(None, None, "stream", "span"),
            P("stream", None, None, None),
            P(),
        ),
        out_specs=P(None, None, "stream", "span"),
        check_vma=False,
    )
```
